32 devices in a mesh: grp: 2 (over y), seq: 8 (over z, core), sp: 2 (over x), rep: 1.
Axes of the slice: x: 2, y: 2, z: 4, core: 2. Of those that a mesh axis runs over, the one named last changes fastest.
Arguments:
- queries: bfloat16 [32, 192, 2048], P(('grp', 'sp', 'seq'), 'rep'), parts along dimension 0, may hold values from -8 to 8
- keys: bfloat16 [32, 192, 2048], P(('grp', 'sp', 'seq'), 'rep'), parts along dimension 0, may hold values from -6 to 6
- values: bfloat16 [32, 192, 2048], P(('grp', 'sp', 'seq'), 'rep'), parts along dimension 0, may hold values from -16 to 16
- text_keys: bfloat16 [512, 2048], P('grp'), parts along dimension 0, may hold values from -6 to 6
- text_values: bfloat16 [512, 2048], P('grp'), parts along dimension 0, may hold values from -16 to 16
- text_count: int32 [2], P('grp'), parts along dimension 0, may hold values from 128 to 256
Outputs:
- attended: bfloat16 [32, 192, 2048], P(('grp', 'sp', 'seq'), 'rep'), parts along dimension 0
The draws below stay inside these ranges and needn't reach their ends.
There are 2 independent parts, one for each index of `grp`. The reference program is written for one: setup_inputs(seed, part) draws one part's arguments, and reference() takes and returns one part's arrays. A program takes and returns all parts, laid end to end along the dimension named above; each array names one. Nothing has to cross between parts.
All inputs are finite; a program needn't handle non-finite values.
Results may differ from the reference program's by a relative error of at most 0.0035.
Values may be sent and summed in bfloat16 or wider, within the bound.
A program may use at most 64 MiB of HBM per device.

```python
import math
import jax
import jax.numpy as jnp
from jax import lax

HEADS = 16
HDIM = 128
WIDTH = 2048
TILE = 192
COLS = 4
TILES = 16
TEXT = 256
WIN = 9


def paired_fields(key):
    base = jax.random.fold_in(key, 1234)
    key_query, key_key = jax.random.split(base, 2)
    shape = (TILES, TILE, WIDTH)
    query_field = jnp.clip(jax.random.normal(key_query, shape, jnp.float32) * 2.0, -8.0, 8.0)
    key_field = jnp.clip(jax.random.normal(key_key, shape, jnp.float32), -6.0, 6.0)
    return (query_field, key_field)


def draw_queries(key, part):
    return paired_fields(key)[0].astype(jnp.bfloat16)


def draw_keys(key, part):
    return paired_fields(key)[1].astype(jnp.bfloat16)


def block_levels(key, extent, cuts, least, top_value):
    loudness = 1.0
    for dim, shards_of in cuts:
        steps = jax.random.uniform(jax.random.fold_in(jax.random.fold_in(key, 6), dim), (shards_of,), jnp.float32, least / len(cuts), top_value / len(cuts))
        loudness = loudness * jnp.repeat(jnp.exp(steps), extent[dim] // shards_of).reshape((-1,) + (1,) * (len(extent) - 1 - dim))
    return loudness


def gaussian(rng, shape, scale, reach, pieces=(), kind=jnp.bfloat16):
    level = block_levels(rng, shape, pieces, -0.22, 0.18) if pieces else 1.0
    values = jax.random.normal(rng, shape, jnp.float32) * scale * level
    return jnp.minimum(jnp.maximum(values, -reach), reach).astype(kind)


def setup_inputs(seed: int = 0, part: int = 0) -> dict:
    key_of = jax.random.split(jax.random.key(seed), 7)
    part_keys = jax.random.split(jax.random.fold_in(key_of[6], part), 7)
    queries = draw_queries(jax.random.fold_in(jax.random.fold_in(key_of[6], part), 71), part)
    keys = draw_keys(jax.random.fold_in(jax.random.fold_in(key_of[6], part), 71), part)
    values = gaussian(part_keys[2], (TILES, TILE, WIDTH), 4.0, 16.0, ((0, 16),))
    text_keys = gaussian(part_keys[3], (TEXT, WIDTH), 1.0, 6.0)
    text_values = gaussian(part_keys[4], (TEXT, WIDTH), 4.0, 16.0)
    text_count = jax.random.randint(part_keys[5], (1,), TEXT // 2, TEXT + 1).astype(jnp.int32)
    return dict(queries=queries, keys=keys, values=values, text_keys=text_keys, text_values=text_values, text_count=text_count)


masked_score = -1e+30

def reference(queries, keys, values, text_keys, text_values, text_count):
    score_scale = 1.0 / math.sqrt(HDIM)
    text_live = jnp.arange(TEXT, dtype=jnp.int32) < text_count[0]
    text_key_rows = text_keys.astype(jnp.float32).reshape(TEXT, HEADS, HDIM)
    text_val_rows = text_values.astype(jnp.float32).reshape(TEXT, HEADS, HDIM)
    position = jnp.arange(WIN, dtype=jnp.int32)
    col_step = position % 3 - 1
    shifts = (position // 3 - 1) * COLS + col_step

    def one_tile(tile_num):
        targets = tile_num + shifts
        column = tile_num % COLS + col_step
        inside = (targets >= 0) & (targets < TILES) & (column >= 0) & (column < COLS)
        safe = jnp.clip(targets, 0, TILES - 1).astype(jnp.int32)
        near_keys = keys[safe].astype(jnp.float32).reshape(WIN * TILE, HEADS, HDIM)
        near_values = values[safe].astype(jnp.float32).reshape(WIN * TILE, HEADS, HDIM)
        query_rows = queries[tile_num].astype(jnp.float32).reshape(TILE, HEADS, HDIM)
        img_scores = jnp.einsum('qhd,khd->hqk', query_rows, near_keys) * score_scale
        img_scores = jnp.where(jnp.repeat(inside, TILE)[None, None, :], img_scores, masked_score)
        txt_scores = jnp.einsum('qhd,khd->hqk', query_rows, text_key_rows) * score_scale
        txt_scores = jnp.where(text_live[None, None, :], txt_scores, masked_score)
        row_top = jnp.maximum(lax.optimization_barrier(jnp.max(img_scores, axis=-1)), lax.optimization_barrier(jnp.max(txt_scores, axis=-1)))
        img_exp = jnp.exp(img_scores - row_top[..., None])
        txt_exp = jnp.exp(txt_scores - row_top[..., None])
        row_total = lax.optimization_barrier(jnp.sum(img_exp, axis=-1)) + lax.optimization_barrier(jnp.sum(txt_exp, axis=-1))
        img_weights = lax.optimization_barrier(img_exp.astype(jnp.bfloat16)).astype(jnp.float32)
        txt_weights = lax.optimization_barrier(txt_exp.astype(jnp.bfloat16)).astype(jnp.float32)
        summed = jnp.einsum('hqk,khd->qhd', img_weights, near_values)
        summed = summed + jnp.einsum('hqk,khd->qhd', txt_weights, text_val_rows)
        summed = summed / jnp.transpose(row_total)[:, :, None]
        return summed.reshape(TILE, WIDTH).astype(jnp.bfloat16)
    return lax.map(one_tile, jnp.arange(TILES, dtype=jnp.int32))
```

```python
import functools
import math

import jax
import jax.numpy as jnp
from jax import lax
from jax.experimental import pallas as pl
from jax.experimental.pallas import tpu as pltpu
from jax.sharding import PartitionSpec as P

HEADS = 16
HDIM = 128
COLS = 4
WIN = 9
REACH = 5


masked_score = -1e30


def with_halo(cells, sides, width):
    for axis, dim in sides:
        count = lax.axis_size(axis)
        ends = count - 1
        head = lax.slice_in_dim(cells, 0, width, axis=dim)
        tail = lax.slice_in_dim(cells, cells.shape[dim] - width, cells.shape[dim], axis=dim)
        cells = jnp.concatenate(
            [
                lax.ppermute(tail, axis, [(i, (i + 1) % count) for i in range(ends)]),
                cells,
                lax.ppermute(head, axis, [((i + 1) % count, i) for i in range(ends)]),
            ],
            axis=dim,
        )
    return cells


def attend(q_here, padded, text_kv, text_count, base_tile, total_tiles, per_dev):
    slab, sub_rows, head_w = q_here.shape
    tile_len = padded.shape[1]
    group_size = 1
    while (
        group_size < slab
        and group_size * sub_rows * per_dev < 512
        and (slab % (2 * group_size) == 0)
    ):
        group_size = group_size * 2
    blocks = slab // group_size
    score_scale = 1.0 / math.sqrt(HDIM)
    text_len = text_kv.shape[0]
    text_key_rows = text_kv[:, 0].reshape(text_len, per_dev, HDIM)
    text_val_rows = text_kv[:, 1].reshape(text_len, per_dev, HDIM)
    text_live = jnp.arange(text_len, dtype=jnp.int32) < text_count[0]
    position = jnp.arange(WIN, dtype=jnp.int32)
    col_step = position % 3 - 1
    shifts = (position // 3 - 1) * COLS + col_step

    def one_group(members):
        block_q, local_tiles = members
        picked = (local_tiles[:, None] + shifts[None, :] + REACH).reshape(-1)
        window_kv = jnp.take(padded, picked, axis=0).reshape(
            group_size, WIN * tile_len, 2, per_dev, HDIM
        )
        win_keys = window_kv[:, :, 0]
        win_values = window_kv[:, :, 1]
        img_scores = (
            jnp.einsum("gqhd,gkhd->ghqk", block_q, win_keys, preferred_element_type=jnp.float32)
            * score_scale
        )
        own_tile = base_tile + local_tiles
        global_tile = own_tile[:, None] + shifts[None, :]
        column = (own_tile % COLS)[:, None] + col_step[None, :]
        valid_tile = (
            (global_tile >= 0) & (global_tile < total_tiles) & (column >= 0) & (column < COLS)
        )
        valid_keys = jnp.repeat(valid_tile, tile_len, axis=1)[:, None, None, :]
        img_scores = jnp.where(valid_keys, img_scores, masked_score)
        txt_scores = (
            jnp.einsum("gqhd,khd->ghqk", block_q, text_key_rows, preferred_element_type=jnp.float32)
            * score_scale
        )
        txt_scores = jnp.where(text_live[None, None, None, :], txt_scores, masked_score)
        row_top = jnp.maximum(jnp.max(img_scores, axis=-1), jnp.max(txt_scores, axis=-1))
        img_exp = jnp.exp(img_scores - row_top[..., None])
        txt_exp = jnp.exp(txt_scores - row_top[..., None])
        row_total = jnp.sum(img_exp, axis=-1) + jnp.sum(txt_exp, axis=-1)
        summed = jnp.einsum(
            "ghqk,gkhd->gqhd",
            img_exp.astype(jnp.bfloat16),
            win_values,
            preferred_element_type=jnp.float32,
        )
        summed = summed + jnp.einsum(
            "ghqk,khd->gqhd",
            txt_exp.astype(jnp.bfloat16),
            text_val_rows,
            preferred_element_type=jnp.float32,
        )
        summed = summed / jnp.transpose(row_total, (0, 2, 1))[..., None]
        return summed.astype(jnp.bfloat16).reshape(group_size, sub_rows, head_w)

    members = (
        q_here.reshape(blocks, group_size, sub_rows, per_dev, HDIM),
        jnp.arange(slab, dtype=jnp.int32).reshape(blocks, group_size),
    )
    return lax.map(one_group, members).reshape(slab, sub_rows, head_w)


def body(queries, keys, values, text_keys, text_values, text_count):
    seq_count = lax.axis_size("seq")
    seq_index = lax.axis_index("seq")
    sp_index = lax.axis_index("sp")
    copies = max(seq_count // HEADS, 1)
    per_dev = max(HEADS // seq_count, 1)
    groups = HEADS // per_dev
    tiles_here, token_half, width = queries.shape
    head_w = per_dev * HDIM
    sub_rows = token_half // copies
    q_items = queries.reshape(tiles_here, copies, sub_rows, groups, head_w)
    q_items = q_items.transpose(3, 1, 0, 2, 4).reshape(seq_count, tiles_here, sub_rows, head_w)
    my_group = seq_index // copies
    text_pair = jnp.stack([text_keys, text_values], axis=1)
    text_kv = lax.dynamic_slice_in_dim(text_pair, my_group * head_w, head_w, 2)
    pair_kv = jnp.stack([keys, values], axis=2)
    length = pair_kv.shape[1]
    kv_items = pair_kv.reshape(tiles_here, length, 2, groups, head_w).transpose(3, 0, 1, 2, 4)
    kv_items = jnp.repeat(kv_items, copies, axis=0)
    q_got, kv_got = (
        lax.all_to_all(q_items, "seq", split_axis=0, concat_axis=1, tiled=True),
        lax.all_to_all(kv_items, "seq", split_axis=0, concat_axis=1, tiled=True),
    )
    q_here = q_got[0]
    kv_here = kv_got[0]
    kv_here = lax.all_gather(kv_here, "rep", axis=1, tiled=True)
    padded = with_halo(kv_here, (("sp", 0),), REACH)
    slab = q_here.shape[0]
    total_tiles = lax.axis_size("sp") * slab
    base_tile = sp_index * slab
    result = attend(q_here, padded, text_kv, text_count, base_tile, total_tiles, per_dev)
    returned = lax.all_to_all(result[None], "seq", split_axis=1, concat_axis=0, tiled=True)
    returned = returned.reshape(groups, copies, tiles_here, sub_rows, head_w).transpose(
        2, 1, 3, 0, 4
    )
    return returned.reshape(tiles_here, token_half, width)


def role_place(role, lines):
    return role // (2 * lines), role // 2 % lines, role % 2


def route(lines):
    count = 4 * lines

    def needs(tile, slab, pos):
        frame, first = divmod((slab * lines + pos) * 2, COLS)
        first = min(max(first - 1, 0), COLS - 3)
        return abs(tile // COLS - frame) <= 1 and first <= tile % COLS <= first + 2

    masks = {}
    depths = {}
    for tile in range(count):
        home_slab, home_pos, home_core = role_place(tile, lines)
        wanted = [needs(tile, 0, p) or needs(tile, 1, p) for p in range(lines)]
        low = min([p for p in range(lines) if wanted[p]] + [home_pos])
        high = max([p for p in range(lines) if wanted[p]] + [home_pos])
        for role in range(count):
            slab, pos, core = role_place(role, lines)
            crossed = slab != home_slab
            moved = core != home_core
            on_line = low <= pos <= high and not crossed and not moved
            on_slab = low <= pos <= high and crossed and not moved and needs(tile, slab, pos)
            on_core = moved and needs(tile, slab, pos)
            acts = []
            if on_line:
                if home_pos <= pos < high:
                    acts.append("up")
                if low < pos <= home_pos:
                    acts.append("down")
                if needs(tile, 1 - slab, pos):
                    acts.append("slab")
            if (on_line or on_slab) and needs(tile, slab, pos):
                acts.append("core")
            if (on_line or on_slab or on_core) and role != tile:
                acts.append("take")
            delta = role ^ tile
            depth = abs(pos - home_pos) + crossed + moved
            for act in acts:
                if act == "take":
                    key = (depth, delta)
                    depths[key] = depths.get(key, 0) | 1 << role
                else:
                    key = (delta, act)
                    masks[key] = masks.get(key, 0) | 1 << role
    return masks, depths


def tile_kernel(
    lines, heads_in, ahead, count_ref, q_hbm, k_hbm, v_hbm, tk_hbm, tv_hbm, o_hbm,
    pairs, q_all, tk_all, tv_all, o_all, bias, text_bias,
    own_sem, side_sem, out_sem, recv_sem, send_sem,
):
    chunks = pairs.shape[0]
    tile_len = pairs.shape[3]
    cols = pairs.shape[4]
    masks, depths = route(lines)
    slab = lax.axis_index("sp")
    spot = lax.axis_index("seq")
    pos = spot // 2
    core = spot % 2
    role = slab * (2 * lines) + spot

    def holds(mask):
        return jnp.right_shift(jnp.int32(mask), role) % 2 == 1

    def tile_at(delta):
        kt = 1 - core if delta & 1 else core
        pt = pos
        if delta & 2:
            pt = pt + 1 - 2 * (pos % 2)
        if delta & 4:
            pt = pt + 2 - 4 * (pos // 2)
        st = 1 - slab if delta & 8 else slab
        return st * (2 * lines) + pt * 2 + kt

    targets = {
        "up": {"seq": spot + 2},
        "down": {"seq": spot - 2},
        "slab": {"sp": 1 - slab},
        "core": {"seq": pos * 2 + 1 - core},
    }
    kinds = ("up", "down", "slab", "core")

    def own_copies(j):
        window = pl.ds(pl.multiple_of(j * cols, cols), cols)
        return [
            pltpu.make_async_copy(k_hbm.at[0, :, window], pairs.at[j, role, 0], own_sem.at[j, 0]),
            pltpu.make_async_copy(v_hbm.at[0, :, window], pairs.at[j, role, 1], own_sem.at[j, 1]),
        ]

    side = [
        pltpu.make_async_copy(q_hbm.at[0], q_all, side_sem.at[0]),
        pltpu.make_async_copy(tk_hbm, tk_all, side_sem.at[1]),
        pltpu.make_async_copy(tv_hbm, tv_all, side_sem.at[2]),
    ]

    for j in range(chunks):
        for copy in own_copies(j):
            copy.start()
    for copy in side:
        copy.start()

    barrier = pltpu.get_barrier_semaphore()

    def greet(kind):
        pl.semaphore_signal(
            barrier, inc=1, device_id=targets[kind], device_id_type=pl.DeviceIdType.MESH
        )

    has_up = pos < lines - 1
    has_down = pos > 0
    greet("core")
    greet("slab")
    pl.when(has_up)(lambda: greet("up"))
    pl.when(has_down)(lambda: greet("down"))
    pl.semaphore_wait(barrier, 2 + has_up.astype(jnp.int32) + has_down.astype(jnp.int32))

    def remote(kind, src, delta, tile, recv):
        return pltpu.make_async_remote_copy(
            src_ref=src,
            dst_ref=src,
            send_sem=send_sem.at[delta, kinds.index(kind)],
            recv_sem=recv,
            device_id=targets[kind],
            device_id_type=pl.DeviceIdType.MESH,
        )

    def pass_on(delta, j):
        tile = tile_at(delta)
        for kind in kinds:
            mask = masks.get((delta, kind), 0)
            if mask:

                @pl.when(holds(mask))
                def _():
                    remote(kind, pairs.at[j, tile], delta, tile, recv_sem.at[tile, j]).start()

    def send_own(j):
        for copy in own_copies(j):
            copy.wait()
        pass_on(0, j)

    def take(delta, mask, j):
        tile = tile_at(delta)

        @pl.when(holds(mask))
        def _():
            remote("core", pairs.at[j, tile], delta, tile, recv_sem.at[tile, j]).wait_recv()
            pass_on(delta, j)

    for j in range(ahead):
        send_own(j)

    frames = 4 * lines // COLS
    frame = role // COLS
    column = role % COLS
    first = jnp.clip(pos * 2 % COLS - 1, 0, COLS - 3)
    starts = []
    lane_tile = lax.broadcasted_iota(jnp.int32, (8, 3 * tile_len), 1) // tile_len + first
    near = (lane_tile >= column - 1) & (lane_tile <= column + 1)
    for step in (-1, 0, 1):
        other = frame + step
        inside = (other >= 0) & (other < frames)
        starts.append(jnp.where(inside, other, frame) * COLS + first)
        live = near & jnp.broadcast_to(inside, near.shape)
        bias[step + 1] = jnp.where(live, 0.0, masked_score).astype(jnp.float32)
    text_len = tk_all.shape[0]
    lane_text = lax.broadcasted_iota(jnp.int32, (8, text_len), 1)
    text_bias[...] = jnp.where(lane_text < count_ref[0], 0.0, masked_score).astype(jnp.float32)
    for copy in side:
        copy.wait()

    factor = math.log2(math.e) / math.sqrt(HDIM)
    turn = (((1,), (1,)), ((), ()))

    def attend_chunk(j):
        for head in range(heads_in):
            inner = slice(head * HDIM, (head + 1) * HDIM)
            outer = pl.ds(pl.multiple_of(j * cols + head * HDIM, HDIM), HDIM)
            q = q_all[:, outer]
            scores = []
            for n, start in enumerate(starts):
                k = pairs[j, pl.ds(start, 3), 0, :, inner].reshape(3 * tile_len, HDIM)
                s = lax.dot_general(q, k, turn, preferred_element_type=jnp.float32)
                scores.append(s + bias[n, 0:1])
            s = lax.dot_general(q, tk_all[:, outer], turn, preferred_element_type=jnp.float32)
            scores.append(s + text_bias[0:1])
            top = functools.reduce(
                jnp.maximum, [jnp.max(s, axis=1, keepdims=True) for s in scores]
            )
            total = 0.0
            summed = 0.0
            for n, s in enumerate(scores):
                w = jnp.exp2((s - top) * factor)
                total = total + jnp.sum(w, axis=1, keepdims=True)
                if n < len(starts):
                    v = pairs[j, pl.ds(starts[n], 3), 1, :, inner].reshape(3 * tile_len, HDIM)
                else:
                    v = tv_all[:, outer]
                summed = summed + jnp.dot(
                    w.astype(jnp.bfloat16), v, preferred_element_type=jnp.float32
                )
            o_all[:, outer] = (summed / total).astype(o_all.dtype)

    def out_copy(j):
        window = pl.ds(pl.multiple_of(j * cols, cols), cols)
        return pltpu.make_async_copy(o_all.at[:, window], o_hbm.at[0, :, window], out_sem.at[j])

    order = sorted(depths)

    def step(j, carry):
        pl.when(j + ahead < chunks)(lambda: send_own(j + ahead))
        for depth, delta in order:
            take(delta, depths[(depth, delta)], j)
        attend_chunk(j)
        out_copy(j).start()
        return carry

    lax.fori_loop(0, chunks, step, 0)

    for (delta, kind), mask in sorted(masks.items()):
        tile = tile_at(delta)

        @pl.when(holds(mask))
        def _():
            remote(kind, pairs.at[:, tile], delta, tile, recv_sem.at[tile, 0]).wait_send()

    for j in range(chunks):
        out_copy(j).wait()


HEADS_IN = 2
AHEAD = 2


def relay_body(queries, keys, values, text_keys, text_values, text_count):
    tile_len, width = queries.shape[1:]
    text_len = text_keys.shape[0]
    lines = lax.axis_size("seq") // 2
    roles = lax.axis_size("sp") * lax.axis_size("seq")
    cols = HEADS_IN * HDIM
    chunks = width // cols
    anywhere = pl.BlockSpec(memory_space=pl.ANY)
    kept = queries.dtype
    return pl.pallas_call(
        functools.partial(tile_kernel, lines, HEADS_IN, AHEAD),
        out_shape=jax.ShapeDtypeStruct(queries.shape, kept),
        in_specs=[pl.BlockSpec(memory_space=pltpu.SMEM)] + [anywhere] * 5,
        out_specs=anywhere,
        scratch_shapes=[
            pltpu.VMEM((chunks, roles, 2, tile_len, cols), kept),
            pltpu.VMEM((tile_len, width), kept),
            pltpu.VMEM((text_len, width), kept),
            pltpu.VMEM((text_len, width), kept),
            pltpu.VMEM((tile_len, width), kept),
            pltpu.VMEM((3, 8, 3 * tile_len), jnp.float32),
            pltpu.VMEM((8, text_len), jnp.float32),
            pltpu.SemaphoreType.DMA((chunks, 2)),
            pltpu.SemaphoreType.DMA((3,)),
            pltpu.SemaphoreType.DMA((chunks,)),
            pltpu.SemaphoreType.DMA((roles, chunks)),
            pltpu.SemaphoreType.DMA((roles, 4)),
        ],
        compiler_params=pltpu.CompilerParams(
            collective_id=0, has_side_effects=True, vmem_limit_bytes=56 * 1024 * 1024
        ),
    )(text_count, queries, keys, values, text_keys, text_values)


def relays(mesh):
    shape = mesh.shape
    return shape["rep"] == 1 and shape["sp"] == 2 and shape["seq"] == 2 * COLS


def solution(mesh):
    in_specs = (
        P(("grp", "sp", "seq"), "rep", None),
        P(("grp", "sp", "seq"), "rep", None),
        P(("grp", "sp", "seq"), "rep", None),
        P("grp", None),
        P("grp", None),
        P("grp"),
    )
    out_specs = P(("grp", "sp", "seq"), "rep", None)
    def chosen(*arrays):
        if relays(mesh) and arrays[0].shape[0] == 1:
            return relay_body(*arrays)
        return body(*arrays)

    return jax.shard_map(chosen, mesh=mesh, in_specs=in_specs, out_specs=out_specs, check_vma=False)
```

```python
import functools
import math

import jax
import jax.numpy as jnp
from jax import lax
from jax.experimental import pallas as pl
from jax.experimental.pallas import tpu as pltpu
from jax.sharding import PartitionSpec as P

HEADS = 16
HDIM = 128
COLS = 4
WIN = 9
REACH = 5


masked_score = -1e30


def with_halo(cells, sides, width):
    for axis, dim in sides:
        count = lax.axis_size(axis)
        ends = count - 1
        head = lax.slice_in_dim(cells, 0, width, axis=dim)
        tail = lax.slice_in_dim(cells, cells.shape[dim] - width, cells.shape[dim], axis=dim)
        cells = jnp.concatenate(
            [
                lax.ppermute(tail, axis, [(i, (i + 1) % count) for i in range(ends)]),
                cells,
                lax.ppermute(head, axis, [((i + 1) % count, i) for i in range(ends)]),
            ],
            axis=dim,
        )
    return cells


def attend(q_here, padded, text_kv, text_count, base_tile, total_tiles, per_dev):
    slab, sub_rows, head_w = q_here.shape
    tile_len = padded.shape[1]
    group_size = 1
    while (
        group_size < slab
        and group_size * sub_rows * per_dev < 512
        and (slab % (2 * group_size) == 0)
    ):
        group_size = group_size * 2
    blocks = slab // group_size
    score_scale = 1.0 / math.sqrt(HDIM)
    text_len = text_kv.shape[0]
    text_key_rows = text_kv[:, 0].reshape(text_len, per_dev, HDIM)
    text_val_rows = text_kv[:, 1].reshape(text_len, per_dev, HDIM)
    text_live = jnp.arange(text_len, dtype=jnp.int32) < text_count[0]
    position = jnp.arange(WIN, dtype=jnp.int32)
    col_step = position % 3 - 1
    shifts = (position // 3 - 1) * COLS + col_step

    def one_group(members):
        block_q, local_tiles = members
        picked = (local_tiles[:, None] + shifts[None, :] + REACH).reshape(-1)
        window_kv = jnp.take(padded, picked, axis=0).reshape(
            group_size, WIN * tile_len, 2, per_dev, HDIM
        )
        win_keys = window_kv[:, :, 0]
        win_values = window_kv[:, :, 1]
        img_scores = (
            jnp.einsum("gqhd,gkhd->ghqk", block_q, win_keys, preferred_element_type=jnp.float32)
            * score_scale
        )
        own_tile = base_tile + local_tiles
        global_tile = own_tile[:, None] + shifts[None, :]
        column = (own_tile % COLS)[:, None] + col_step[None, :]
        valid_tile = (
            (global_tile >= 0) & (global_tile < total_tiles) & (column >= 0) & (column < COLS)
        )
        valid_keys = jnp.repeat(valid_tile, tile_len, axis=1)[:, None, None, :]
        img_scores = jnp.where(valid_keys, img_scores, masked_score)
        txt_scores = (
            jnp.einsum("gqhd,khd->ghqk", block_q, text_key_rows, preferred_element_type=jnp.float32)
            * score_scale
        )
        txt_scores = jnp.where(text_live[None, None, None, :], txt_scores, masked_score)
        row_top = jnp.maximum(jnp.max(img_scores, axis=-1), jnp.max(txt_scores, axis=-1))
        img_exp = jnp.exp(img_scores - row_top[..., None])
        txt_exp = jnp.exp(txt_scores - row_top[..., None])
        row_total = jnp.sum(img_exp, axis=-1) + jnp.sum(txt_exp, axis=-1)
        summed = jnp.einsum(
            "ghqk,gkhd->gqhd",
            img_exp.astype(jnp.bfloat16),
            win_values,
            preferred_element_type=jnp.float32,
        )
        summed = summed + jnp.einsum(
            "ghqk,khd->gqhd",
            txt_exp.astype(jnp.bfloat16),
            text_val_rows,
            preferred_element_type=jnp.float32,
        )
        summed = summed / jnp.transpose(row_total, (0, 2, 1))[..., None]
        return summed.astype(jnp.bfloat16).reshape(group_size, sub_rows, head_w)

    members = (
        q_here.reshape(blocks, group_size, sub_rows, per_dev, HDIM),
        jnp.arange(slab, dtype=jnp.int32).reshape(blocks, group_size),
    )
    return lax.map(one_group, members).reshape(slab, sub_rows, head_w)


def body(queries, keys, values, text_keys, text_values, text_count):
    seq_count = lax.axis_size("seq")
    seq_index = lax.axis_index("seq")
    sp_index = lax.axis_index("sp")
    copies = max(seq_count // HEADS, 1)
    per_dev = max(HEADS // seq_count, 1)
    groups = HEADS // per_dev
    tiles_here, token_half, width = queries.shape
    head_w = per_dev * HDIM
    sub_rows = token_half // copies
    q_items = queries.reshape(tiles_here, copies, sub_rows, groups, head_w)
    q_items = q_items.transpose(3, 1, 0, 2, 4).reshape(seq_count, tiles_here, sub_rows, head_w)
    my_group = seq_index // copies
    text_pair = jnp.stack([text_keys, text_values], axis=1)
    text_kv = lax.dynamic_slice_in_dim(text_pair, my_group * head_w, head_w, 2)
    pair_kv = jnp.stack([keys, values], axis=2)
    length = pair_kv.shape[1]
    kv_items = pair_kv.reshape(tiles_here, length, 2, groups, head_w).transpose(3, 0, 1, 2, 4)
    kv_items = jnp.repeat(kv_items, copies, axis=0)
    q_got, kv_got = (
        lax.all_to_all(q_items, "seq", split_axis=0, concat_axis=1, tiled=True),
        lax.all_to_all(kv_items, "seq", split_axis=0, concat_axis=1, tiled=True),
    )
    q_here = q_got[0]
    kv_here = kv_got[0]
    kv_here = lax.all_gather(kv_here, "rep", axis=1, tiled=True)
    padded = with_halo(kv_here, (("sp", 0),), REACH)
    slab = q_here.shape[0]
    total_tiles = lax.axis_size("sp") * slab
    base_tile = sp_index * slab
    result = attend(q_here, padded, text_kv, text_count, base_tile, total_tiles, per_dev)
    returned = lax.all_to_all(result[None], "seq", split_axis=1, concat_axis=0, tiled=True)
    returned = returned.reshape(groups, copies, tiles_here, sub_rows, head_w).transpose(
        2, 1, 3, 0, 4
    )
    return returned.reshape(tiles_here, token_half, width)


def role_place(role, lines):
    return role // (2 * lines), role // 2 % lines, role % 2


def route(lines):
    count = 4 * lines

    def needs(tile, slab, pos):
        frame, first = divmod((slab * lines + pos) * 2, COLS)
        first = min(max(first - 1, 0), COLS - 3)
        return abs(tile // COLS - frame) <= 1 and first <= tile % COLS <= first + 2

    masks = {}
    depths = {}
    for tile in range(count):
        home_slab, home_pos, home_core = role_place(tile, lines)
        wanted = [needs(tile, 0, p) or needs(tile, 1, p) for p in range(lines)]
        low = min([p for p in range(lines) if wanted[p]] + [home_pos])
        high = max([p for p in range(lines) if wanted[p]] + [home_pos])
        for role in range(count):
            slab, pos, core = role_place(role, lines)
            crossed = slab != home_slab
            moved = core != home_core
            on_line = low <= pos <= high and not crossed and not moved
            on_slab = low <= pos <= high and crossed and not moved and needs(tile, slab, pos)
            on_core = moved and needs(tile, slab, pos)
            acts = []
            if on_line:
                if home_pos <= pos < high:
                    acts.append("up")
                if low < pos <= home_pos:
                    acts.append("down")
                if needs(tile, 1 - slab, pos):
                    acts.append("slab")
            if (on_line or on_slab) and needs(tile, slab, pos):
                acts.append("core")
            if (on_line or on_slab or on_core) and role != tile:
                acts.append("take")
            delta = role ^ tile
            depth = abs(pos - home_pos) + crossed + moved
            for act in acts:
                if act == "take":
                    key = (depth, delta)
                    depths[key] = depths.get(key, 0) | 1 << role
                else:
                    key = (delta, act)
                    masks[key] = masks.get(key, 0) | 1 << role
    return masks, depths


def tile_kernel(
    lines, heads_in, ahead, count_ref, q_hbm, k_hbm, v_hbm, tk_hbm, tv_hbm, o_hbm,
    pairs, q_all, tk_all, tv_all, o_all, bias, text_bias,
    own_sem, side_sem, out_sem, recv_sem, send_sem,
):
    chunks = pairs.shape[0]
    tile_len = pairs.shape[3]
    cols = pairs.shape[4]
    masks, depths = route(lines)
    slab = lax.axis_index("sp")
    spot = lax.axis_index("seq")
    pos = spot // 2
    core = spot % 2
    role = slab * (2 * lines) + spot

    def holds(mask):
        return jnp.right_shift(jnp.int32(mask), role) % 2 == 1

    def tile_at(delta):
        kt = 1 - core if delta & 1 else core
        pt = pos
        if delta & 2:
            pt = pt + 1 - 2 * (pos % 2)
        if delta & 4:
            pt = pt + 2 - 4 * (pos // 2)
        st = 1 - slab if delta & 8 else slab
        return st * (2 * lines) + pt * 2 + kt

    targets = {
        "up": {"seq": spot + 2},
        "down": {"seq": spot - 2},
        "slab": {"sp": 1 - slab},
        "core": {"seq": pos * 2 + 1 - core},
    }
    kinds = ("up", "down", "slab", "core")

    def own_copies(j):
        window = pl.ds(pl.multiple_of(j * cols, cols), cols)
        return [
            pltpu.make_async_copy(k_hbm.at[0, :, window], pairs.at[j, role, 0], own_sem.at[j, 0]),
            pltpu.make_async_copy(v_hbm.at[0, :, window], pairs.at[j, role, 1], own_sem.at[j, 1]),
        ]

    side = [
        pltpu.make_async_copy(q_hbm.at[0], q_all, side_sem.at[0]),
        pltpu.make_async_copy(tk_hbm, tk_all, side_sem.at[1]),
        pltpu.make_async_copy(tv_hbm, tv_all, side_sem.at[2]),
    ]

    for j in range(chunks):
        for copy in own_copies(j):
            copy.start()
    for copy in side:
        copy.start()

    barrier = pltpu.get_barrier_semaphore()

    def greet(kind):
        pl.semaphore_signal(
            barrier, inc=1, device_id=targets[kind], device_id_type=pl.DeviceIdType.MESH
        )

    has_up = pos < lines - 1
    has_down = pos > 0
    greet("core")
    greet("slab")
    pl.when(has_up)(lambda: greet("up"))
    pl.when(has_down)(lambda: greet("down"))
    pl.semaphore_wait(barrier, 2 + has_up.astype(jnp.int32) + has_down.astype(jnp.int32))

    def remote(kind, src, delta, tile, recv):
        return pltpu.make_async_remote_copy(
            src_ref=src,
            dst_ref=src,
            send_sem=send_sem.at[delta, kinds.index(kind)],
            recv_sem=recv,
            device_id=targets[kind],
            device_id_type=pl.DeviceIdType.MESH,
        )

    def pass_on(delta, j):
        tile = tile_at(delta)
        for kind in kinds:
            mask = masks.get((delta, kind), 0)
            if mask:

                @pl.when(holds(mask))
                def _():
                    remote(kind, pairs.at[j, tile], delta, tile, recv_sem.at[tile, j]).start()

    def send_own(j):
        for copy in own_copies(j):
            copy.wait()
        pass_on(0, j)

    def take(delta, mask, j):
        tile = tile_at(delta)

        @pl.when(holds(mask))
        def _():
            remote("core", pairs.at[j, tile], delta, tile, recv_sem.at[tile, j]).wait_recv()
            pass_on(delta, j)

    for j in range(ahead):
        send_own(j)

    frames = 4 * lines // COLS
    frame = role // COLS
    column = role % COLS
    first = jnp.clip(pos * 2 % COLS - 1, 0, COLS - 3)
    starts = []
    lane_tile = lax.broadcasted_iota(jnp.int32, (8, 3 * tile_len), 1) // tile_len + first
    near = (lane_tile >= column - 1) & (lane_tile <= column + 1)
    for step in (-1, 0, 1):
        other = frame + step
        inside = (other >= 0) & (other < frames)
        starts.append(jnp.where(inside, other, frame) * COLS + first)
        live = near & jnp.broadcast_to(inside, near.shape)
        bias[step + 1] = jnp.where(live, 0.0, masked_score).astype(jnp.float32)
    text_len = tk_all.shape[0]
    lane_text = lax.broadcasted_iota(jnp.int32, (8, text_len), 1)
    text_bias[...] = jnp.where(lane_text < count_ref[0], 0.0, masked_score).astype(jnp.float32)
    for copy in side:
        copy.wait()

    factor = math.log2(math.e) / math.sqrt(HDIM)
    turn = (((1,), (1,)), ((), ()))

    def attend_chunk(j):
        for head in range(heads_in):
            inner = slice(head * HDIM, (head + 1) * HDIM)
            outer = pl.ds(pl.multiple_of(j * cols + head * HDIM, HDIM), HDIM)
            q = q_all[:, outer]
            scores = []
            for n, start in enumerate(starts):
                k = pairs[j, pl.ds(start, 3), 0, :, inner].reshape(3 * tile_len, HDIM)
                s = lax.dot_general(q, k, turn, preferred_element_type=jnp.float32)
                scores.append(s + bias[n, 0:1])
            s = lax.dot_general(q, tk_all[:, outer], turn, preferred_element_type=jnp.float32)
            scores.append(s + text_bias[0:1])
            top = functools.reduce(
                jnp.maximum, [jnp.max(s, axis=1, keepdims=True) for s in scores]
            )
            total = 0.0
            summed = 0.0
            for n, s in enumerate(scores):
                w = jnp.exp2((s - top) * factor)
                total = total + jnp.sum(w, axis=1, keepdims=True)
                if n < len(starts):
                    v = pairs[j, pl.ds(starts[n], 3), 1, :, inner].reshape(3 * tile_len, HDIM)
                else:
                    v = tv_all[:, outer]
                summed = summed + jnp.dot(
                    w.astype(jnp.bfloat16), v, preferred_element_type=jnp.float32
                )
            o_all[:, outer] = (summed / total).astype(o_all.dtype)

    def out_copy(j):
        window = pl.ds(pl.multiple_of(j * cols, cols), cols)
        return pltpu.make_async_copy(o_all.at[:, window], o_hbm.at[0, :, window], out_sem.at[j])

    order = sorted(depths)
    deepest = order[-1][0]

    def step(s, carry):
        pl.when(s + ahead < chunks)(lambda: send_own(s + ahead))
        for depth in range(1, deepest + 1):
            j = s - (depth - 1)

            @pl.when((j >= 0) & (j < chunks))
            def _():
                for at, delta in order:
                    if at == depth:
                        take(delta, depths[(at, delta)], j)

        ready = s - (deepest - 1)

        @pl.when(ready >= 0)
        def _():
            attend_chunk(ready)
            out_copy(ready).start()

        return carry

    lax.fori_loop(0, chunks + deepest - 1, step, 0)

    for (delta, kind), mask in sorted(masks.items()):
        tile = tile_at(delta)

        @pl.when(holds(mask))
        def _():
            remote(kind, pairs.at[:, tile], delta, tile, recv_sem.at[tile, 0]).wait_send()

    for j in range(chunks):
        out_copy(j).wait()


HEADS_IN = 1
AHEAD = 2


def relay_body(queries, keys, values, text_keys, text_values, text_count):
    tile_len, width = queries.shape[1:]
    text_len = text_keys.shape[0]
    lines = lax.axis_size("seq") // 2
    roles = lax.axis_size("sp") * lax.axis_size("seq")
    cols = HEADS_IN * HDIM
    chunks = width // cols
    anywhere = pl.BlockSpec(memory_space=pl.ANY)
    kept = queries.dtype
    return pl.pallas_call(
        functools.partial(tile_kernel, lines, HEADS_IN, AHEAD),
        out_shape=jax.ShapeDtypeStruct(queries.shape, kept),
        in_specs=[pl.BlockSpec(memory_space=pltpu.SMEM)] + [anywhere] * 5,
        out_specs=anywhere,
        scratch_shapes=[
            pltpu.VMEM((chunks, roles, 2, tile_len, cols), kept),
            pltpu.VMEM((tile_len, width), kept),
            pltpu.VMEM((text_len, width), kept),
            pltpu.VMEM((text_len, width), kept),
            pltpu.VMEM((tile_len, width), kept),
            pltpu.VMEM((3, 8, 3 * tile_len), jnp.float32),
            pltpu.VMEM((8, text_len), jnp.float32),
            pltpu.SemaphoreType.DMA((chunks, 2)),
            pltpu.SemaphoreType.DMA((3,)),
            pltpu.SemaphoreType.DMA((chunks,)),
            pltpu.SemaphoreType.DMA((roles, chunks)),
            pltpu.SemaphoreType.DMA((roles, 4)),
        ],
        compiler_params=pltpu.CompilerParams(
            collective_id=0, has_side_effects=True, vmem_limit_bytes=56 * 1024 * 1024
        ),
    )(text_count, queries, keys, values, text_keys, text_values)


def relays(mesh):
    shape = mesh.shape
    return shape["rep"] == 1 and shape["sp"] == 2 and shape["seq"] == 2 * COLS


def solution(mesh):
    in_specs = (
        P(("grp", "sp", "seq"), "rep", None),
        P(("grp", "sp", "seq"), "rep", None),
        P(("grp", "sp", "seq"), "rep", None),
        P("grp", None),
        P("grp", None),
        P("grp"),
    )
    out_specs = P(("grp", "sp", "seq"), "rep", None)
    def chosen(*arrays):
        if relays(mesh) and arrays[0].shape[0] == 1:
            return relay_body(*arrays)
        return body(*arrays)

    return jax.shard_map(chosen, mesh=mesh, in_specs=in_specs, out_specs=out_specs, check_vma=False)
```

```python
import functools
import math

import jax
import jax.numpy as jnp
from jax import lax
from jax.experimental import pallas as pl
from jax.experimental.pallas import tpu as pltpu
from jax.sharding import PartitionSpec as P

HEADS = 16
HDIM = 128
COLS = 4
WIN = 9
REACH = 5


masked_score = -1e30


def with_halo(cells, sides, width):
    for axis, dim in sides:
        count = lax.axis_size(axis)
        ends = count - 1
        head = lax.slice_in_dim(cells, 0, width, axis=dim)
        tail = lax.slice_in_dim(cells, cells.shape[dim] - width, cells.shape[dim], axis=dim)
        cells = jnp.concatenate(
            [
                lax.ppermute(tail, axis, [(i, (i + 1) % count) for i in range(ends)]),
                cells,
                lax.ppermute(head, axis, [((i + 1) % count, i) for i in range(ends)]),
            ],
            axis=dim,
        )
    return cells


def attend(q_here, padded, text_kv, text_count, base_tile, total_tiles, per_dev):
    slab, sub_rows, head_w = q_here.shape
    tile_len = padded.shape[1]
    group_size = 1
    while (
        group_size < slab
        and group_size * sub_rows * per_dev < 512
        and (slab % (2 * group_size) == 0)
    ):
        group_size = group_size * 2
    blocks = slab // group_size
    score_scale = 1.0 / math.sqrt(HDIM)
    text_len = text_kv.shape[0]
    text_key_rows = text_kv[:, 0].reshape(text_len, per_dev, HDIM)
    text_val_rows = text_kv[:, 1].reshape(text_len, per_dev, HDIM)
    text_live = jnp.arange(text_len, dtype=jnp.int32) < text_count[0]
    position = jnp.arange(WIN, dtype=jnp.int32)
    col_step = position % 3 - 1
    shifts = (position // 3 - 1) * COLS + col_step

    def one_group(members):
        block_q, local_tiles = members
        picked = (local_tiles[:, None] + shifts[None, :] + REACH).reshape(-1)
        window_kv = jnp.take(padded, picked, axis=0).reshape(
            group_size, WIN * tile_len, 2, per_dev, HDIM
        )
        win_keys = window_kv[:, :, 0]
        win_values = window_kv[:, :, 1]
        img_scores = (
            jnp.einsum("gqhd,gkhd->ghqk", block_q, win_keys, preferred_element_type=jnp.float32)
            * score_scale
        )
        own_tile = base_tile + local_tiles
        global_tile = own_tile[:, None] + shifts[None, :]
        column = (own_tile % COLS)[:, None] + col_step[None, :]
        valid_tile = (
            (global_tile >= 0) & (global_tile < total_tiles) & (column >= 0) & (column < COLS)
        )
        valid_keys = jnp.repeat(valid_tile, tile_len, axis=1)[:, None, None, :]
        img_scores = jnp.where(valid_keys, img_scores, masked_score)
        txt_scores = (
            jnp.einsum("gqhd,khd->ghqk", block_q, text_key_rows, preferred_element_type=jnp.float32)
            * score_scale
        )
        txt_scores = jnp.where(text_live[None, None, None, :], txt_scores, masked_score)
        row_top = jnp.maximum(jnp.max(img_scores, axis=-1), jnp.max(txt_scores, axis=-1))
        img_exp = jnp.exp(img_scores - row_top[..., None])
        txt_exp = jnp.exp(txt_scores - row_top[..., None])
        row_total = jnp.sum(img_exp, axis=-1) + jnp.sum(txt_exp, axis=-1)
        summed = jnp.einsum(
            "ghqk,gkhd->gqhd",
            img_exp.astype(jnp.bfloat16),
            win_values,
            preferred_element_type=jnp.float32,
        )
        summed = summed + jnp.einsum(
            "ghqk,khd->gqhd",
            txt_exp.astype(jnp.bfloat16),
            text_val_rows,
            preferred_element_type=jnp.float32,
        )
        summed = summed / jnp.transpose(row_total, (0, 2, 1))[..., None]
        return summed.astype(jnp.bfloat16).reshape(group_size, sub_rows, head_w)

    members = (
        q_here.reshape(blocks, group_size, sub_rows, per_dev, HDIM),
        jnp.arange(slab, dtype=jnp.int32).reshape(blocks, group_size),
    )
    return lax.map(one_group, members).reshape(slab, sub_rows, head_w)


def body(queries, keys, values, text_keys, text_values, text_count):
    seq_count = lax.axis_size("seq")
    seq_index = lax.axis_index("seq")
    sp_index = lax.axis_index("sp")
    copies = max(seq_count // HEADS, 1)
    per_dev = max(HEADS // seq_count, 1)
    groups = HEADS // per_dev
    tiles_here, token_half, width = queries.shape
    head_w = per_dev * HDIM
    sub_rows = token_half // copies
    q_items = queries.reshape(tiles_here, copies, sub_rows, groups, head_w)
    q_items = q_items.transpose(3, 1, 0, 2, 4).reshape(seq_count, tiles_here, sub_rows, head_w)
    my_group = seq_index // copies
    text_pair = jnp.stack([text_keys, text_values], axis=1)
    text_kv = lax.dynamic_slice_in_dim(text_pair, my_group * head_w, head_w, 2)
    pair_kv = jnp.stack([keys, values], axis=2)
    length = pair_kv.shape[1]
    kv_items = pair_kv.reshape(tiles_here, length, 2, groups, head_w).transpose(3, 0, 1, 2, 4)
    kv_items = jnp.repeat(kv_items, copies, axis=0)
    q_got, kv_got = (
        lax.all_to_all(q_items, "seq", split_axis=0, concat_axis=1, tiled=True),
        lax.all_to_all(kv_items, "seq", split_axis=0, concat_axis=1, tiled=True),
    )
    q_here = q_got[0]
    kv_here = kv_got[0]
    kv_here = lax.all_gather(kv_here, "rep", axis=1, tiled=True)
    padded = with_halo(kv_here, (("sp", 0),), REACH)
    slab = q_here.shape[0]
    total_tiles = lax.axis_size("sp") * slab
    base_tile = sp_index * slab
    result = attend(q_here, padded, text_kv, text_count, base_tile, total_tiles, per_dev)
    returned = lax.all_to_all(result[None], "seq", split_axis=1, concat_axis=0, tiled=True)
    returned = returned.reshape(groups, copies, tiles_here, sub_rows, head_w).transpose(
        2, 1, 3, 0, 4
    )
    return returned.reshape(tiles_here, token_half, width)


def role_place(role, lines):
    return role // (2 * lines), role // 2 % lines, role % 2


def route(lines):
    count = 4 * lines

    def needs(tile, slab, pos):
        frame, first = divmod((slab * lines + pos) * 2, COLS)
        first = min(max(first - 1, 0), COLS - 3)
        return abs(tile // COLS - frame) <= 1 and first <= tile % COLS <= first + 2

    masks = {}
    depths = {}
    for tile in range(count):
        home_slab, home_pos, home_core = role_place(tile, lines)
        wanted = [needs(tile, 0, p) or needs(tile, 1, p) for p in range(lines)]
        low = min([p for p in range(lines) if wanted[p]] + [home_pos])
        high = max([p for p in range(lines) if wanted[p]] + [home_pos])
        for role in range(count):
            slab, pos, core = role_place(role, lines)
            crossed = slab != home_slab
            moved = core != home_core
            on_line = low <= pos <= high and not crossed and not moved
            on_slab = low <= pos <= high and crossed and not moved and needs(tile, slab, pos)
            on_core = moved and needs(tile, slab, pos)
            acts = []
            if on_line:
                if home_pos <= pos < high:
                    acts.append("up")
                if low < pos <= home_pos:
                    acts.append("down")
                if needs(tile, 1 - slab, pos):
                    acts.append("slab")
            if (on_line or on_slab) and needs(tile, slab, pos):
                acts.append("core")
            if (on_line or on_slab or on_core) and role != tile:
                acts.append("take")
            delta = role ^ tile
            depth = abs(pos - home_pos) + crossed + moved
            for act in acts:
                if act == "take":
                    key = (depth, delta)
                    depths[key] = depths.get(key, 0) | 1 << role
                else:
                    key = (delta, act)
                    masks[key] = masks.get(key, 0) | 1 << role
    return masks, depths


def tile_kernel(
    lines, heads_in, ahead, count_ref, q_hbm, k_hbm, v_hbm, tk_hbm, tv_hbm, o_hbm,
    pairs, q_all, tk_all, tv_all, o_all, bias, text_bias,
    own_sem, side_sem, out_sem, recv_sem, send_sem,
):
    chunks = pairs.shape[0]
    tile_len = pairs.shape[3]
    cols = pairs.shape[4]
    masks, depths = route(lines)
    slab = lax.axis_index("sp")
    spot = lax.axis_index("seq")
    pos = spot // 2
    core = spot % 2
    role = slab * (2 * lines) + spot

    def holds(mask):
        return jnp.right_shift(jnp.int32(mask), role) % 2 == 1

    def tile_at(delta):
        kt = 1 - core if delta & 1 else core
        pt = pos
        if delta & 2:
            pt = pt + 1 - 2 * (pos % 2)
        if delta & 4:
            pt = pt + 2 - 4 * (pos // 2)
        st = 1 - slab if delta & 8 else slab
        return st * (2 * lines) + pt * 2 + kt

    targets = {
        "up": {"seq": spot + 2},
        "down": {"seq": spot - 2},
        "slab": {"sp": 1 - slab},
        "core": {"seq": pos * 2 + 1 - core},
    }
    kinds = ("up", "down", "slab", "core")

    def own_copies(j):
        window = pl.ds(pl.multiple_of(j * cols, cols), cols)
        return [
            pltpu.make_async_copy(k_hbm.at[0, :, window], pairs.at[j, role, 0], own_sem.at[j, 0]),
            pltpu.make_async_copy(v_hbm.at[0, :, window], pairs.at[j, role, 1], own_sem.at[j, 1]),
        ]

    side = [
        pltpu.make_async_copy(q_hbm.at[0], q_all, side_sem.at[0]),
        pltpu.make_async_copy(tk_hbm, tk_all, side_sem.at[1]),
        pltpu.make_async_copy(tv_hbm, tv_all, side_sem.at[2]),
    ]

    for j in range(chunks):
        for copy in own_copies(j):
            copy.start()
    for copy in side:
        copy.start()

    barrier = pltpu.get_barrier_semaphore()

    def greet(kind):
        pl.semaphore_signal(
            barrier, inc=1, device_id=targets[kind], device_id_type=pl.DeviceIdType.MESH
        )

    has_up = pos < lines - 1
    has_down = pos > 0
    greet("core")
    greet("slab")
    pl.when(has_up)(lambda: greet("up"))
    pl.when(has_down)(lambda: greet("down"))
    pl.semaphore_wait(barrier, 2 + has_up.astype(jnp.int32) + has_down.astype(jnp.int32))

    def remote(kind, src, delta, tile, recv):
        return pltpu.make_async_remote_copy(
            src_ref=src,
            dst_ref=src,
            send_sem=send_sem.at[delta, kinds.index(kind)],
            recv_sem=recv,
            device_id=targets[kind],
            device_id_type=pl.DeviceIdType.MESH,
        )

    def pass_on(delta, j):
        tile = tile_at(delta)
        for kind in kinds:
            mask = masks.get((delta, kind), 0)
            if mask:

                @pl.when(holds(mask))
                def _():
                    remote(kind, pairs.at[j, tile], delta, tile, recv_sem.at[tile, j]).start()

    def send_own(j):
        for copy in own_copies(j):
            copy.wait()
        pass_on(0, j)

    def take(delta, mask, j):
        tile = tile_at(delta)

        @pl.when(holds(mask))
        def _():
            remote("core", pairs.at[j, tile], delta, tile, recv_sem.at[tile, j]).wait_recv()
            pass_on(delta, j)

    for j in range(ahead):
        send_own(j)

    frames = 4 * lines // COLS
    frame = role // COLS
    column = role % COLS
    first = jnp.clip(pos * 2 % COLS - 1, 0, COLS - 3)
    starts = []
    lane_tile = lax.broadcasted_iota(jnp.int32, (8, 3 * tile_len), 1) // tile_len + first
    near = (lane_tile >= column - 1) & (lane_tile <= column + 1)
    for step in (-1, 0, 1):
        other = frame + step
        inside = (other >= 0) & (other < frames)
        starts.append(jnp.where(inside, other, frame) * COLS + first)
        live = near & jnp.broadcast_to(inside, near.shape)
        bias[step + 1] = jnp.where(live, 0.0, masked_score).astype(jnp.float32)
    text_len = tk_all.shape[0]
    lane_text = lax.broadcasted_iota(jnp.int32, (8, text_len), 1)
    text_bias[...] = jnp.where(lane_text < count_ref[0], 0.0, masked_score).astype(jnp.float32)
    for copy in side:
        copy.wait()

    factor = math.log2(math.e) / math.sqrt(HDIM)
    turn = (((1,), (1,)), ((), ()))

    def attend_chunk(j):
        for head in range(heads_in):
            inner = slice(head * HDIM, (head + 1) * HDIM)
            outer = pl.ds(pl.multiple_of(j * cols + head * HDIM, HDIM), HDIM)
            q = q_all[:, outer]
            scores = []
            for n, start in enumerate(starts):
                k = pairs[j, pl.ds(start, 3), 0, :, inner].reshape(3 * tile_len, HDIM)
                s = lax.dot_general(q, k, turn, preferred_element_type=jnp.float32)
                scores.append(s + bias[n, 0:1])
            s = lax.dot_general(q, tk_all[:, outer], turn, preferred_element_type=jnp.float32)
            scores.append(s + text_bias[0:1])
            top = functools.reduce(
                jnp.maximum, [jnp.max(s, axis=1, keepdims=True) for s in scores]
            )
            total = 0.0
            summed = 0.0
            for n, s in enumerate(scores):
                w = jnp.exp2((s - top) * factor)
                total = total + jnp.sum(w, axis=1, keepdims=True)
                if n < len(starts):
                    v = pairs[j, pl.ds(starts[n], 3), 1, :, inner].reshape(3 * tile_len, HDIM)
                else:
                    v = tv_all[:, outer]
                summed = summed + jnp.dot(
                    w.astype(jnp.bfloat16), v, preferred_element_type=jnp.float32
                )
            o_all[:, outer] = (summed / total).astype(o_all.dtype)

    def out_copy(j):
        window = pl.ds(pl.multiple_of(j * cols, cols), cols)
        return pltpu.make_async_copy(o_all.at[:, window], o_hbm.at[0, :, window], out_sem.at[j])

    order = sorted(depths, key=lambda at: (at[0], at[1] % 2, at[1]))
    deepest = order[-1][0]

    def step(s, carry):
        pl.when(s + ahead < chunks)(lambda: send_own(s + ahead))
        for depth in range(1, deepest + 1):
            j = s - (depth - 1)

            @pl.when((j >= 0) & (j < chunks))
            def _():
                for at, delta in order:
                    if at == depth:
                        take(delta, depths[(at, delta)], j)

        ready = s - (deepest - 1)

        @pl.when(ready >= 0)
        def _():
            attend_chunk(ready)
            out_copy(ready).start()

        return carry

    lax.fori_loop(0, chunks + deepest - 1, step, 0)

    for (delta, kind), mask in sorted(masks.items()):
        tile = tile_at(delta)

        @pl.when(holds(mask))
        def _():
            remote(kind, pairs.at[:, tile], delta, tile, recv_sem.at[tile, 0]).wait_send()

    for j in range(chunks):
        out_copy(j).wait()


HEADS_IN = 1
AHEAD = 1


def relay_body(queries, keys, values, text_keys, text_values, text_count):
    tile_len, width = queries.shape[1:]
    text_len = text_keys.shape[0]
    lines = lax.axis_size("seq") // 2
    roles = lax.axis_size("sp") * lax.axis_size("seq")
    cols = HEADS_IN * HDIM
    chunks = width // cols
    anywhere = pl.BlockSpec(memory_space=pl.ANY)
    kept = queries.dtype
    return pl.pallas_call(
        functools.partial(tile_kernel, lines, HEADS_IN, AHEAD),
        out_shape=jax.ShapeDtypeStruct(queries.shape, kept),
        in_specs=[pl.BlockSpec(memory_space=pltpu.SMEM)] + [anywhere] * 5,
        out_specs=anywhere,
        scratch_shapes=[
            pltpu.VMEM((chunks, roles, 2, tile_len, cols), kept),
            pltpu.VMEM((tile_len, width), kept),
            pltpu.VMEM((text_len, width), kept),
            pltpu.VMEM((text_len, width), kept),
            pltpu.VMEM((tile_len, width), kept),
            pltpu.VMEM((3, 8, 3 * tile_len), jnp.float32),
            pltpu.VMEM((8, text_len), jnp.float32),
            pltpu.SemaphoreType.DMA((chunks, 2)),
            pltpu.SemaphoreType.DMA((3,)),
            pltpu.SemaphoreType.DMA((chunks,)),
            pltpu.SemaphoreType.DMA((roles, chunks)),
            pltpu.SemaphoreType.DMA((roles, 4)),
        ],
        compiler_params=pltpu.CompilerParams(
            collective_id=0, has_side_effects=True, vmem_limit_bytes=56 * 1024 * 1024
        ),
    )(text_count, queries, keys, values, text_keys, text_values)


def relays(mesh):
    shape = mesh.shape
    return shape["rep"] == 1 and shape["sp"] == 2 and shape["seq"] == 2 * COLS


def solution(mesh):
    in_specs = (
        P(("grp", "sp", "seq"), "rep", None),
        P(("grp", "sp", "seq"), "rep", None),
        P(("grp", "sp", "seq"), "rep", None),
        P("grp", None),
        P("grp", None),
        P("grp"),
    )
    out_specs = P(("grp", "sp", "seq"), "rep", None)
    def chosen(*arrays):
        if relays(mesh) and arrays[0].shape[0] == 1:
            return relay_body(*arrays)
        return body(*arrays)

    return jax.shard_map(chosen, mesh=mesh, in_specs=in_specs, out_specs=out_specs, check_vma=False)
```
